32 devices in a mesh: row: 8 (over z, y), col: 4 (over x, core).
Axes of the slice: x: 2, y: 2, z: 4, core: 2. Of those that a mesh axis runs over, the one named last changes fastest.
Arguments:
- gradient: bfloat16 [512, 28672], P('col', 'row'), may hold values from -6 to 6
- basis: bfloat16 [28672, 28672], P('row', 'col'), may hold values from -0.03125 to 0.03125
- eigen: float32 [512, 28672], P('row', 'col'), may hold values from 0.2 to 5
Outputs:
- result: bfloat16 [512, 28672], P('col', 'row')
The draws below stay inside these ranges and needn't reach their ends.
All inputs are finite; a program needn't handle non-finite values.
Results may differ from the reference program's by a relative error of at most 0.0044.
Values may be sent and summed in bfloat16 or wider, within the bound.
No kernel may reach another device: no remote copies, remote signals or barrier semaphores. Data moves between devices by JAX's collectives and lax.ppermute only.
A program may use at most 128 MiB of HBM per device.

```python
import math
import jax
import jax.numpy as jnp
from jax import lax

FF = 28672
ROWS = 512
N_COL = 4


def block_scale(key, dims, pieces, smallest, largest):
    def one(position, blocks):
        steps = jax.random.uniform(jax.random.fold_in(jax.random.fold_in(key, 6), position), (blocks,), jnp.float32, smallest / len(pieces), largest / len(pieces))
        return jnp.repeat(jnp.exp(steps), dims[position] // blocks).reshape((-1,) + (1,) * (len(dims) - position - 1))

    loudness = one(*pieces[0])
    for cut in pieces[1:]:
        loudness = loudness * one(*cut)
    return loudness


def centred(key, shape, deviation, most, split=(), kind=jnp.bfloat16):
    array = jax.random.normal(key, shape, jnp.float32) * deviation
    if len(split) > 0:
        array = block_scale(key, shape, split, -0.22, 0.18) * array
    return jnp.clip(array, min=-most, max=most).astype(kind)


def setup_inputs(seed: int = 0) -> dict:
    keys = jax.random.split(jax.random.key(seed), 4)
    return {
        "gradient": centred(keys[0], (ROWS, FF), 1.0, 6.0, ((0, 4), (1, 8))),
        "basis": centred(keys[1], (FF, FF), FF ** -0.5, 0.03125, ((0, 8), (1, 4))),
        "eigen": jnp.clip(jnp.exp(math.log(5.0) - 3.218876 * jax.random.uniform(keys[2], (ROWS, FF), jnp.float32) ** block_scale(keys[2], (ROWS, FF), ((0, 8), (1, 4)), -0.2, 0.2)), 0.2, 5.0),
    }


def reference(gradient, basis, eigen):
    width = FF // N_COL
    grad_float = gradient.astype(jnp.float32)

    def rotate_block(index):
        start = (index * width).astype(jnp.int32)
        block = lax.dynamic_slice_in_dim(basis, start, width, 1).astype(jnp.float32)
        return jnp.dot(grad_float, block, precision=lax.Precision.HIGHEST)

    blocks = lax.map(rotate_block, jnp.arange(N_COL, dtype=jnp.int32))
    rotated = jnp.concatenate([blocks[i] for i in range(N_COL)], axis=1)
    scaled = (rotated / eigen).astype(jnp.bfloat16).astype(jnp.float32)

    def back_block(index):
        start = (index * width).astype(jnp.int32)
        block = lax.dynamic_slice_in_dim(basis, start, width, 0).astype(jnp.float32)
        return jnp.dot(scaled, block.T, precision=lax.Precision.HIGHEST)

    backs = lax.map(back_block, jnp.arange(N_COL, dtype=jnp.int32))
    result = jnp.concatenate([backs[i] for i in range(N_COL)], axis=1)
    return result.astype(jnp.bfloat16)
```

```python
import functools

import jax
import jax.numpy as jnp
from jax import lax
from jax.experimental import pallas as pl
from jax.experimental.pallas import tpu as pltpu
from jax.sharding import PartitionSpec as P


F32, BF16 = jnp.float32, jnp.bfloat16
LANES = 128
ALONG = (((1,), (1,)), ((), ()))


def swap(x, axis, size, bit):
    return lax.ppermute(x, axis, [(d, d ^ (1 << bit)) for d in range(size)])


def tile_of(width, most):
    tiles = width // LANES
    return LANES * max(n for n in range(1, most // LANES + 1) if tiles % n == 0)


def pick(x, index, axis):
    return lax.dynamic_index_in_dim(x, index, axis, keepdims=False)


def in_order(mine, other, bit, axis):
    mine, other = jnp.expand_dims(mine, axis), jnp.expand_dims(other, axis)
    low = jnp.concatenate([mine, other], axis)
    high = jnp.concatenate([other, mine], axis)
    return jnp.where(bit == 0, low, high)


def general(n_row, n_col, gradient, basis, eigen):
    row_bits, col_bits = n_row.bit_length() - 1, n_col.bit_length() - 1
    r, c = lax.axis_index("row"), lax.axis_index("col")
    rbit = [(r >> b) & 1 for b in range(row_bits)]
    cbit = [(c >> b) & 1 for b in range(col_bits)]
    block = eigen.shape[0]
    w = tile_of(basis.shape[1], basis.shape[1] // 4)
    count = basis.shape[1] // w

    whole, have = gradient, []
    for b in reversed(range(col_bits)):
        got = swap(whole, "col", n_col, b)
        have = sorted(have + [b], reverse=True)
        whole = in_order(whole, got, cbit[b], have.index(b))
    whole = whole.reshape((2,) * row_bits + (block, -1))
    order = list(range(row_bits))
    k = whole.shape[-1]
    sends = pick(whole, 1 - rbit[0], row_bits - 1).reshape(-1, k)
    keeps = pick(whole, rbit[0], row_bits - 1).reshape(-1, k)

    scaled = []
    for i in range(count):
        cols = basis[:, i * w : (i + 1) * w]
        left = list(reversed(order[1:]))
        shape = (2,) * len(left) + (block, w)
        away = jnp.dot(sends, cols, preferred_element_type=F32).astype(BF16)
        mine = jnp.dot(keeps, cols, preferred_element_type=F32).reshape(shape)
        for b in order[1:]:
            total = mine + swap(away, "row", n_row, b - 1).reshape(mine.shape).astype(F32)
            axis = left.index(b)
            away, mine = pick(total, 1 - rbit[b], axis).astype(BF16), pick(total, rbit[b], axis)
            left.remove(b)
        total = mine + swap(away, "row", n_row, order[-1]).reshape(mine.shape).astype(F32)
        part, have = (total / eigen[:, i * w : (i + 1) * w]).astype(BF16), []
        for b in reversed(order):
            got = swap(part, "row", n_row, b)
            have = sorted(have + [b], reverse=True)
            part = in_order(part, got, rbit[b], have.index(b))
        scaled.append(part.reshape(n_row * block, w))

    out = None
    for i in range(count):
        cols = basis[:, i * w : (i + 1) * w]
        term = lax.dot_general(scaled[i], cols, ALONG, preferred_element_type=F32)
        out = term if out is None else out + term
    out = out.reshape((2,) * col_bits + (gradient.shape[0], -1))
    left = list(reversed(range(col_bits)))
    for b in range(col_bits):
        axis = left.index(b)
        away, mine = pick(out, 1 - cbit[b], axis).astype(BF16), pick(out, cbit[b], axis)
        out = mine + swap(away, "col", n_col, b).astype(F32)
        left.remove(b)
    return out.astype(BF16)


def copy_block(sources, which, at, rows, to, slot):
    at = pl.multiple_of(at * rows, rows)
    for d, source in enumerate(sources):

        @pl.when(which == d)
        def _():
            to[pl.ds(slot * rows, rows), :] = source[pl.ds(at, rows), :]


def rotate_body(bits, block, n, idx, *refs):
    shards, (b, away, keep, rows) = refs[:n], refs[n:]
    slots = 1 << len(bits)

    @pl.when(pl.program_id(0) == 0)
    def _():
        for slot in range(slots):
            p = {bit: slot >> (len(bits) - 1 - j) & 1 for j, bit in enumerate(bits)}
            which = idx[1] ^ p[1]
            if 2 in p:
                which = which + 2 * (idx[2] ^ p[2])
            copy_block(shards, which, idx[0] ^ p[0], block, rows, slot)

    out = jnp.dot(rows[...], b[...], preferred_element_type=F32)
    half = slots // 2 * block
    keep[...] = out[:half]
    away[...] = out[half:].astype(BF16)


def fixed(shape):
    return pl.BlockSpec(shape, lambda i, idx: (0, 0), pipeline_mode=pl.Buffered(1))


def rotate(idx, shards, basis, start, w, bits, block):
    k = shards[0].shape[1]
    tile = tile_of(w, 896)
    first = start // tile
    count = block << len(bits)
    rows = pl.BlockSpec((count // 2, tile), lambda i, idx: (0, i))
    return pl.pallas_call(
        functools.partial(rotate_body, bits, block, len(shards)),
        grid_spec=pltpu.PrefetchScalarGridSpec(
            num_scalar_prefetch=1,
            grid=(w // tile,),
            in_specs=[fixed(x.shape) for x in shards]
            + [pl.BlockSpec((k, tile), lambda i, idx: (0, i + first))],
            out_specs=[rows, rows],
            scratch_shapes=[pltpu.VMEM((count, k), BF16)],
        ),
        out_shape=[
            jax.ShapeDtypeStruct((count // 2, w), BF16),
            jax.ShapeDtypeStruct((count // 2, w), F32),
        ],
        compiler_params=pltpu.CompilerParams(vmem_limit_bytes=30 << 20),
        cost_estimate=pl.CostEstimate(
            flops=2 * count * k * w, bytes_accessed=2 * k * w, transcendentals=0
        ),
        name="rotate",
    )(idx, *shards, basis)


def back_body(bits, block, more, idx, lo, hi, b, *refs):
    parts = 1 << len(bits) - 1
    rows, outs, before = refs[-1], refs[-1 - parts : -1], refs[:parts]

    @pl.when(pl.program_id(0) == 0)
    def _():
        for slot in range(2 * parts):
            p = {bit: idx[bit] ^ (slot >> bit & 1) for bit in bits}
            at = p[bits[1]] if len(bits) == 2 else 2 * p[bits[1]] + p[bits[2]]
            copy_block((lo, hi), p[bits[0]], at, block, rows, slot)

    out = lax.dot_general(rows[...], b[...], ALONG, preferred_element_type=F32)
    for n in range(parts):
        part = out[2 * n * block : 2 * (n + 1) * block]
        if more:
            part = part + before[n][...]
        outs[n][...] = part.astype(outs[n].dtype)


def back(idx, lo, hi, basis, start, w, bits, block, before, last):
    k = basis.shape[0]
    tile = tile_of(k, 896)
    rows = pl.BlockSpec((2 * block, tile), lambda i, idx: (0, i))
    parts = 1 << len(bits) - 1
    return pl.pallas_call(
        functools.partial(back_body, bits, block, len(before) > 0),
        grid_spec=pltpu.PrefetchScalarGridSpec(
            num_scalar_prefetch=1,
            grid=(k // tile,),
            in_specs=[
                fixed(lo.shape),
                fixed(hi.shape),
                pl.BlockSpec((tile, w), lambda i, idx: (i, start // w)),
            ]
            + [rows] * len(before),
            out_specs=[rows] * parts,
            scratch_shapes=[pltpu.VMEM((2 * lo.shape[0], w), BF16)],
        ),
        out_shape=[
            jax.ShapeDtypeStruct((2 * block, k), BF16 if last and n % 2 else F32)
            for n in range(parts)
        ],
        compiler_params=pltpu.CompilerParams(vmem_limit_bytes=24 << 20),
        cost_estimate=pl.CostEstimate(
            flops=4 * lo.shape[0] * k * w, bytes_accessed=2 * k * w, transcendentals=0
        ),
        name="back",
    )(idx, lo, hi, basis, *before)


def columns(body, idx, ins, outs):
    w = outs[0].shape[1]
    tile = tile_of(w, 1792)
    specs = [
        pl.BlockSpec((x.shape[0], tile), functools.partial(lambda f, i, idx: (0, i + f), start // tile))
        for x, start in ins
    ]
    moved = sum(x.shape[0] * w * x.dtype.itemsize for x, _ in ins)
    return pl.pallas_call(
        body,
        grid_spec=pltpu.PrefetchScalarGridSpec(
            num_scalar_prefetch=1,
            grid=(w // tile,),
            in_specs=specs,
            out_specs=[pl.BlockSpec((o.shape[0], tile), lambda i, idx: (0, i)) for o in outs],
        ),
        out_shape=outs,
        compiler_params=pltpu.CompilerParams(vmem_limit_bytes=24 << 20),
        cost_estimate=pl.CostEstimate(flops=moved, bytes_accessed=2 * moved, transcendentals=0),
    )(idx, *[x for x, _ in ins])


def sum_body(idx, keep, got, away):
    away[...] = (keep[...] + got[...].astype(F32)).astype(BF16)


def three(keep, a, b, rows):
    return keep[rows, :] + a[rows, :].astype(F32) + b[rows, :].astype(F32)


def halve_body(idx, keep, got, more, keep2, away2):
    half = keep2.shape[0]
    keep2[...] = three(keep, got, more, slice(0, half))
    away2[...] = three(keep, got, more, slice(half, 2 * half)).astype(BF16)


def merge_body(idx, own, own_y, own_e, far, far_y, far_e, keep, away):
    a = three(own, own_y, own_e, slice(None))
    b = three(far, far_y, far_e, slice(None))
    straight = idx[2] == 0
    keep[...] = jnp.where(straight, a, b)
    away[...] = jnp.where(straight, b, a).astype(BF16)


def scale_body(idx, keep, got, mine, other, out):
    block = mine.shape[0]
    low = idx[3] == 0
    total = keep[...] + got[...].astype(F32)
    first = jnp.where(low, mine[...], other[...])
    second = jnp.where(low, other[...], mine[...])
    out[:block, :] = (total[:block] / first).astype(BF16)
    out[block:, :] = (total[block:] / second).astype(BF16)


def inner(idx, a, b):
    return jnp.where(idx[4] == 1, a[...], b[...])


def join_body(idx, near, away, near_out, away_out, out):
    half = near.shape[0]
    out[:half, :] = inner(idx, near, near_out)
    out[half:, :] = inner(idx, away, away_out)


def part_body(idx, near, away, near_out, away_out, own, far):
    a, b = inner(idx, near, near_out), inner(idx, away, away_out)
    straight = idx[2] == 0
    own[...] = jnp.where(straight, a, b)
    far[...] = jnp.where(straight, b, a)


def add_body(idx, keep, got, out):
    out[...] = (keep[...] + got[...].astype(F32)).astype(BF16)


def last_body(idx, keep, got, far, out):
    out[...] = (keep[...] + got[...].astype(F32) + far[...].astype(F32)).astype(BF16)


def paired(n_row, n_col, chunks, gradient, basis, eigen):
    r, c = lax.axis_index("row"), lax.axis_index("col")
    bits = [r & 1, c & 1, ((r >> 2) ^ (c >> 1)) & 1, (r >> 1) & 1, ((r >> 2) ^ (r >> 1)) & 1]
    idx = jnp.stack(bits).astype(jnp.int32)
    block = eigen.shape[0]
    w = eigen.shape[1] // len(chunks)
    s = jax.ShapeDtypeStruct
    mid = [d for d in range(n_row) if (d >> 2 ^ d >> 1) & 1]
    inwards = [(d ^ 2, d) for d in mid]
    outwards = [(d, d ^ 2) for d in mid]
    across = [(d, d ^ 6) for d in mid]

    def send(x, pairs):
        return lax.ppermute(x, "row", pairs)

    def row(x):
        return swap(x, "row", n_row, 0)

    def col(x, bit):
        return swap(x, "col", n_col, bit)

    def cols(body, ins, outs):
        ins = [x if isinstance(x, tuple) else (x, 0) for x in ins]
        outs = [s((rows, w), kind) for rows, kind in outs]
        out = columns(body, idx, ins, outs)
        return out if len(outs) > 1 else out[0]

    far_half = col(gradient, 1)
    shards = {"own": (gradient, col(gradient, 0)), "far": (far_half, col(far_half, 0))}
    other = send(eigen, inwards)

    def rotated(held, start, order):
        away, keep = rotate(idx, held, basis, start, w, order, block)
        got = row(away)
        total = cols(sum_body, [keep, got], [(keep.shape[0], BF16)])
        return [keep, got, send(total, inwards)]

    held = {}
    halves = [(2 * block, F32), (2 * block, BF16)]
    for i, (cut, _) in enumerate(chunks):
        if cut:
            part = rotated(shards["own"], i * w, (0, 1))
            part += rotated(shards["far"], i * w, (0, 1))
            keep, away = cols(merge_body, part, halves)
        else:
            part = rotated(shards["own"] + shards["far"], i * w, (0, 2, 1))
            keep, away = cols(halve_body, part, halves)
        got = send(away, across)
        held[i] = cols(scale_body, [keep, got, (eigen, i * w), (other, i * w)], halves[1:])

    done = ()
    for i, (_, cut) in enumerate(chunks):
        near = held[i]
        away = send(near, across)
        near_out = send(near, outwards)
        parts = [near, away, near_out, send(away, outwards)]
        last = i == len(chunks) - 1
        if not cut:
            lo = cols(join_body, parts, [(4 * block, BF16)])
            hi = row(lo)
            done = back(idx, lo, hi, basis, i * w, w, (0, 2, 1), block, done, last)
            continue
        own, far = cols(part_body, parts, [(2 * block, BF16)] * 2)
        parts = []
        for lo, before in ((own, done[:2]), (far, done[2:])):
            hi = row(lo)
            parts += back(idx, lo, hi, basis, i * w, w, (0, 1), block, before, last)
        done = tuple(parts)

    def final(body, ins):
        outs = [s(gradient.shape, BF16)]
        return columns(body, idx, [(x, 0) for x in ins], outs)[0]

    far = final(add_body, [done[2], col(done[3], 0)])
    far = col(far, 1)
    return final(last_body, [done[0], col(done[1], 0), far])


CHUNKS = (
    (True, False),
    (True, False),
    (False, True),
    (False, True),
)


def solution(mesh):
    n_row, n_col = mesh.shape["row"], mesh.shape["col"]
    fits = n_row == 2 * n_col and n_col.bit_length() == 3

    def per_device(gradient, basis, eigen):
        if fits:
            return paired(n_row, n_col, CHUNKS, gradient, basis, eigen)
        return general(n_row, n_col, gradient, basis, eigen)

    return jax.shard_map(
        per_device,
        mesh=mesh,
        in_specs=(P("col", "row"), P("row", "col"), P("row", "col")),
        out_specs=P("col", "row"),
        check_vma=False,
    )
```

```python
import functools

import jax
import jax.numpy as jnp
from jax import lax
from jax.experimental import pallas as pl
from jax.experimental.pallas import tpu as pltpu
from jax.sharding import PartitionSpec as P


F32, BF16 = jnp.float32, jnp.bfloat16
LANES = 128
ALONG = (((1,), (1,)), ((), ()))


def swap(x, axis, size, bit):
    return lax.ppermute(x, axis, [(d, d ^ (1 << bit)) for d in range(size)])


def tile_of(width, most):
    tiles = width // LANES
    return LANES * max(n for n in range(1, most // LANES + 1) if tiles % n == 0)


def pick(x, index, axis):
    return lax.dynamic_index_in_dim(x, index, axis, keepdims=False)


def in_order(mine, other, bit, axis):
    mine, other = jnp.expand_dims(mine, axis), jnp.expand_dims(other, axis)
    low = jnp.concatenate([mine, other], axis)
    high = jnp.concatenate([other, mine], axis)
    return jnp.where(bit == 0, low, high)


def general(n_row, n_col, gradient, basis, eigen):
    row_bits, col_bits = n_row.bit_length() - 1, n_col.bit_length() - 1
    r, c = lax.axis_index("row"), lax.axis_index("col")
    rbit = [(r >> b) & 1 for b in range(row_bits)]
    cbit = [(c >> b) & 1 for b in range(col_bits)]
    block = eigen.shape[0]
    w = tile_of(basis.shape[1], basis.shape[1] // 4)
    count = basis.shape[1] // w

    whole, have = gradient, []
    for b in reversed(range(col_bits)):
        got = swap(whole, "col", n_col, b)
        have = sorted(have + [b], reverse=True)
        whole = in_order(whole, got, cbit[b], have.index(b))
    whole = whole.reshape((2,) * row_bits + (block, -1))
    order = list(range(row_bits))
    k = whole.shape[-1]
    sends = pick(whole, 1 - rbit[0], row_bits - 1).reshape(-1, k)
    keeps = pick(whole, rbit[0], row_bits - 1).reshape(-1, k)

    scaled = []
    for i in range(count):
        cols = basis[:, i * w : (i + 1) * w]
        left = list(reversed(order[1:]))
        shape = (2,) * len(left) + (block, w)
        away = jnp.dot(sends, cols, preferred_element_type=F32).astype(BF16)
        mine = jnp.dot(keeps, cols, preferred_element_type=F32).reshape(shape)
        for b in order[1:]:
            total = mine + swap(away, "row", n_row, b - 1).reshape(mine.shape).astype(F32)
            axis = left.index(b)
            away, mine = pick(total, 1 - rbit[b], axis).astype(BF16), pick(total, rbit[b], axis)
            left.remove(b)
        total = mine + swap(away, "row", n_row, order[-1]).reshape(mine.shape).astype(F32)
        part, have = (total / eigen[:, i * w : (i + 1) * w]).astype(BF16), []
        for b in reversed(order):
            got = swap(part, "row", n_row, b)
            have = sorted(have + [b], reverse=True)
            part = in_order(part, got, rbit[b], have.index(b))
        scaled.append(part.reshape(n_row * block, w))

    out = None
    for i in range(count):
        cols = basis[:, i * w : (i + 1) * w]
        term = lax.dot_general(scaled[i], cols, ALONG, preferred_element_type=F32)
        out = term if out is None else out + term
    out = out.reshape((2,) * col_bits + (gradient.shape[0], -1))
    left = list(reversed(range(col_bits)))
    for b in range(col_bits):
        axis = left.index(b)
        away, mine = pick(out, 1 - cbit[b], axis).astype(BF16), pick(out, cbit[b], axis)
        out = mine + swap(away, "col", n_col, b).astype(F32)
        left.remove(b)
    return out.astype(BF16)


def copy_block(sources, which, at, rows, to, slot):
    at = pl.multiple_of(at * rows, rows)
    for d, source in enumerate(sources):

        @pl.when(which == d)
        def _():
            to[pl.ds(slot * rows, rows), :] = source[pl.ds(at, rows), :]


DEPTH = 4


def stream(steps, fetch, work):
    def prime(_=None):
        for i in range(min(DEPTH - 1, steps)):
            fetch(i, i).start()

    def loop():
        def step(i, carry):
            slot = lax.rem(i, DEPTH)
            fetch(i, slot).wait()

            @pl.when(i + DEPTH - 1 < steps)
            def _():
                fetch(i + DEPTH - 1, lax.rem(i + DEPTH - 1, DEPTH)).start()

            work(i, slot)
            return carry

        lax.fori_loop(0, steps, step, 0)

    return prime, loop


def rotate_body(bits, block, n, start, tile, idx, *refs):
    shards, (b, away, keep, rows, ring, sems) = refs[:n], refs[n:]
    slots = 1 << len(bits)
    half = slots // 2 * block

    def fetch(i, slot):
        at = pl.multiple_of(start + i * tile, LANES)
        return pltpu.make_async_copy(b.at[:, pl.ds(at, tile)], ring.at[slot], sems.at[slot])

    def work(i, slot):
        out = jnp.dot(rows[...], ring[slot], preferred_element_type=F32)
        at = pl.ds(pl.multiple_of(i * tile, LANES), tile)
        keep[:, at] = out[:half]
        away[:, at] = out[half:].astype(BF16)

    prime, loop = stream(keep.shape[1] // tile, fetch, work)
    prime()
    for slot in range(slots):
        p = {bit: slot >> (len(bits) - 1 - j) & 1 for j, bit in enumerate(bits)}
        which = idx[1] ^ p[1]
        if 2 in p:
            which = which + 2 * (idx[2] ^ p[2])
        copy_block(shards, which, idx[0] ^ p[0], block, rows, slot)
    loop()


VMEM = pl.BlockSpec(memory_space=pltpu.VMEM)


def kernel(body, outs, scratch, aliases, flops, moved, limit, idx, basis_at, *args):
    specs = [pl.BlockSpec(memory_space=pltpu.SMEM)] + [VMEM] * len(args)
    specs[1 + basis_at] = pl.BlockSpec(memory_space=pl.ANY)
    return pl.pallas_call(
        body,
        in_specs=specs,
        out_specs=[VMEM] * len(outs),
        out_shape=outs,
        scratch_shapes=scratch + [pltpu.SemaphoreType.DMA((DEPTH,))],
        input_output_aliases=aliases,
        compiler_params=pltpu.CompilerParams(vmem_limit_bytes=limit),
        cost_estimate=pl.CostEstimate(flops=flops, bytes_accessed=moved, transcendentals=0),
    )(idx, *args)


def rotate(idx, shards, basis, start, w, bits, block):
    k = shards[0].shape[1]
    tile = tile_of(w, 256)
    count = block << len(bits)
    return kernel(
        functools.partial(rotate_body, bits, block, len(shards), start, tile),
        [jax.ShapeDtypeStruct((count // 2, w), x) for x in (BF16, F32)],
        [pltpu.VMEM((count, k), BF16), pltpu.VMEM((DEPTH, k, tile), BF16)],
        {},
        2 * count * k * w,
        2 * k * w,
        26 << 20,
        idx,
        len(shards),
        *shards,
        basis,
    )


def back_body(bits, block, more, start, tile, idx, lo, hi, b, *refs):
    parts = 1 << len(bits) - 1
    before = refs[:parts]
    outs, (rows, ring, sems) = refs[-3 - parts : -3], refs[-3:]
    w = lo.shape[1]

    def fetch(i, slot):
        at = pl.ds(pl.multiple_of(i * tile, tile), tile)
        return pltpu.make_async_copy(b.at[at, pl.ds(start, w)], ring.at[slot], sems.at[slot])

    def work(i, slot):
        out = lax.dot_general(rows[...], ring[slot], ALONG, preferred_element_type=F32)
        at = pl.ds(pl.multiple_of(i * tile, LANES), tile)
        for n in range(parts):
            part = out[2 * n * block : 2 * (n + 1) * block]
            if more:
                part = part + before[n][:, at]
            outs[n][:, at] = part.astype(outs[n].dtype)

    prime, loop = stream(b.shape[0] // tile, fetch, work)
    prime()
    for slot in range(2 * parts):
        p = {bit: idx[bit] ^ (slot >> bit & 1) for bit in bits}
        at = p[bits[1]] if len(bits) == 2 else 2 * p[bits[1]] + p[bits[2]]
        copy_block((lo, hi), p[bits[0]], at, block, rows, slot)
    loop()


def back(idx, lo, hi, basis, start, w, bits, block, before, last):
    k = basis.shape[0]
    tile = tile_of(k, 512)
    parts = 1 << len(bits) - 1
    kinds = [BF16 if last and n % 2 else F32 for n in range(parts)]
    return kernel(
        functools.partial(back_body, bits, block, len(before) > 0, start, tile),
        [jax.ShapeDtypeStruct((2 * block, k), x) for x in kinds],
        [pltpu.VMEM((2 * lo.shape[0], w), BF16), pltpu.VMEM((DEPTH, tile, w), BF16)],
        {4 + n: n for n in range(len(before)) if kinds[n] == F32},
        4 * lo.shape[0] * k * w,
        2 * k * w,
        26 << 20,
        idx,
        2,
        lo,
        hi,
        basis,
        *before,
    )


def columns(body, idx, ins, outs):
    w = outs[0].shape[1]
    tile = tile_of(w, 1792)
    specs = [
        pl.BlockSpec((x.shape[0], tile), functools.partial(lambda f, i, idx: (0, i + f), start // tile))
        for x, start in ins
    ]
    moved = sum(x.shape[0] * w * x.dtype.itemsize for x, _ in ins)
    return pl.pallas_call(
        body,
        grid_spec=pltpu.PrefetchScalarGridSpec(
            num_scalar_prefetch=1,
            grid=(w // tile,),
            in_specs=specs,
            out_specs=[pl.BlockSpec((o.shape[0], tile), lambda i, idx: (0, i)) for o in outs],
        ),
        out_shape=outs,
        compiler_params=pltpu.CompilerParams(vmem_limit_bytes=24 << 20),
        cost_estimate=pl.CostEstimate(flops=moved, bytes_accessed=2 * moved, transcendentals=0),
    )(idx, *[x for x, _ in ins])


def sum_body(idx, keep, got, away):
    away[...] = (keep[...] + got[...].astype(F32)).astype(BF16)


def three(keep, a, b, rows):
    return keep[rows, :] + a[rows, :].astype(F32) + b[rows, :].astype(F32)


def halve_body(idx, keep, got, more, keep2, away2):
    half = keep2.shape[0]
    keep2[...] = three(keep, got, more, slice(0, half))
    away2[...] = three(keep, got, more, slice(half, 2 * half)).astype(BF16)


def merge_body(idx, own, own_y, own_e, far, far_y, far_e, keep, away):
    a = three(own, own_y, own_e, slice(None))
    b = three(far, far_y, far_e, slice(None))
    straight = idx[2] == 0
    keep[...] = jnp.where(straight, a, b)
    away[...] = jnp.where(straight, b, a).astype(BF16)


def scale_body(idx, keep, got, mine, other, out):
    block = mine.shape[0]
    low = idx[3] == 0
    total = keep[...] + got[...].astype(F32)
    first = jnp.where(low, mine[...], other[...])
    second = jnp.where(low, other[...], mine[...])
    out[:block, :] = (total[:block] / first).astype(BF16)
    out[block:, :] = (total[block:] / second).astype(BF16)


def inner(idx, a, b):
    return jnp.where(idx[4] == 1, a[...], b[...])


def join_body(idx, near, away, near_out, away_out, out):
    half = near.shape[0]
    out[:half, :] = inner(idx, near, near_out)
    out[half:, :] = inner(idx, away, away_out)


def part_body(idx, near, away, near_out, away_out, own, far):
    a, b = inner(idx, near, near_out), inner(idx, away, away_out)
    straight = idx[2] == 0
    own[...] = jnp.where(straight, a, b)
    far[...] = jnp.where(straight, b, a)


def add_body(idx, keep, got, out):
    out[...] = (keep[...] + got[...].astype(F32)).astype(BF16)


def last_body(idx, keep, got, far, out):
    out[...] = (keep[...] + got[...].astype(F32) + far[...].astype(F32)).astype(BF16)


def paired(n_row, n_col, chunks, gradient, basis, eigen):
    r, c = lax.axis_index("row"), lax.axis_index("col")
    bits = [r & 1, c & 1, ((r >> 2) ^ (c >> 1)) & 1, (r >> 1) & 1, ((r >> 2) ^ (r >> 1)) & 1]
    idx = jnp.stack(bits).astype(jnp.int32)
    block = eigen.shape[0]
    starts, at = [], 0
    for part, _, _ in chunks:
        starts.append(at)
        at += eigen.shape[1] * part // PARTS
    widths = [b - a for a, b in zip(starts, starts[1:] + [at])]
    s = jax.ShapeDtypeStruct
    mid = [d for d in range(n_row) if (d >> 2 ^ d >> 1) & 1]
    inwards = [(d ^ 2, d) for d in mid]
    outwards = [(d, d ^ 2) for d in mid]
    across = [(d, d ^ 6) for d in mid]

    def send(x, pairs):
        return lax.ppermute(x, "row", pairs)

    def row(x):
        return swap(x, "row", n_row, 0)

    def col(x, bit):
        return swap(x, "col", n_col, bit)

    def cols(body, ins, outs):
        ins = [x if isinstance(x, tuple) else (x, 0) for x in ins]
        outs = [s((rows, ins[0][0].shape[1]), kind) for rows, kind in outs]
        out = columns(body, idx, ins, outs)
        return out if len(outs) > 1 else out[0]

    far_half = col(gradient, 1)
    shards = {"own": (gradient, col(gradient, 0)), "far": (far_half, col(far_half, 0))}
    other = send(eigen, inwards)

    def rotated(held, i, order):
        away, keep = rotate(idx, held, basis, starts[i], widths[i], order, block)
        got = row(away)
        total = cols(sum_body, [keep, got], [(keep.shape[0], BF16)])
        return [keep, got, send(total, inwards)]

    held = {}
    halves = [(2 * block, F32), (2 * block, BF16)]
    for i, (_, cut, _) in enumerate(chunks):
        if cut:
            part = rotated(shards["own"], i, (0, 1))
            part += rotated(shards["far"], i, (0, 1))
            keep, away = cols(merge_body, part, halves)
        else:
            part = rotated(shards["own"] + shards["far"], i, (0, 2, 1))
            keep, away = cols(halve_body, part, halves)
        got = send(away, across)
        held[i] = cols(scale_body, [keep, got, (eigen, starts[i]), (other, starts[i])], halves[1:])

    done = ()
    for i, (_, _, cut) in enumerate(chunks):
        near = held[i]
        away = send(near, across)
        near_out = send(near, outwards)
        parts = [near, away, near_out, send(away, outwards)]
        last = i == len(chunks) - 1
        if not cut:
            lo = cols(join_body, parts, [(4 * block, BF16)])
            hi = row(lo)
            done = back(idx, lo, hi, basis, starts[i], widths[i], (0, 2, 1), block, done, last)
            continue
        own, far = cols(part_body, parts, [(2 * block, BF16)] * 2)
        parts = []
        for lo, before in ((own, done[:2]), (far, done[2:])):
            hi = row(lo)
            parts += back(idx, lo, hi, basis, starts[i], widths[i], (0, 1), block, before, last)
        done = tuple(parts)

    def final(body, ins):
        outs = [s(gradient.shape, BF16)]
        return columns(body, idx, [(x, 0) for x in ins], outs)[0]

    far = final(add_body, [done[2], col(done[3], 0)])
    far = col(far, 1)
    return final(last_body, [done[0], col(done[1], 0), far])


CHUNKS = (
    (7, True, False),
    (7, True, False),
    (7, False, True),
    (7, False, True),
)
PARTS = sum(part for part, _, _ in CHUNKS)


def solution(mesh):
    n_row, n_col = mesh.shape["row"], mesh.shape["col"]
    fits = n_row == 2 * n_col and n_col.bit_length() == 3

    def per_device(gradient, basis, eigen):
        if fits:
            return paired(n_row, n_col, CHUNKS, gradient, basis, eigen)
        return general(n_row, n_col, gradient, basis, eigen)

    return jax.shard_map(
        per_device,
        mesh=mesh,
        in_specs=(P("col", "row"), P("row", "col"), P("row", "col")),
        out_specs=P("col", "row"),
        check_vma=False,
    )
```

```python
import functools

import jax
import jax.numpy as jnp
from jax import lax
from jax.experimental import pallas as pl
from jax.experimental.pallas import tpu as pltpu
from jax.sharding import PartitionSpec as P


F32, BF16 = jnp.float32, jnp.bfloat16
LANES = 128
ALONG = (((1,), (1,)), ((), ()))


def swap(x, axis, size, bit):
    return lax.ppermute(x, axis, [(d, d ^ (1 << bit)) for d in range(size)])


def tile_of(width, most):
    tiles = width // LANES
    return LANES * max(n for n in range(1, most // LANES + 1) if tiles % n == 0)


def pick(x, index, axis):
    return lax.dynamic_index_in_dim(x, index, axis, keepdims=False)


def in_order(mine, other, bit, axis):
    mine, other = jnp.expand_dims(mine, axis), jnp.expand_dims(other, axis)
    low = jnp.concatenate([mine, other], axis)
    high = jnp.concatenate([other, mine], axis)
    return jnp.where(bit == 0, low, high)


def general(n_row, n_col, gradient, basis, eigen):
    row_bits, col_bits = n_row.bit_length() - 1, n_col.bit_length() - 1
    r, c = lax.axis_index("row"), lax.axis_index("col")
    rbit = [(r >> b) & 1 for b in range(row_bits)]
    cbit = [(c >> b) & 1 for b in range(col_bits)]
    block = eigen.shape[0]
    w = tile_of(basis.shape[1], basis.shape[1] // 4)
    count = basis.shape[1] // w

    whole, have = gradient, []
    for b in reversed(range(col_bits)):
        got = swap(whole, "col", n_col, b)
        have = sorted(have + [b], reverse=True)
        whole = in_order(whole, got, cbit[b], have.index(b))
    whole = whole.reshape((2,) * row_bits + (block, -1))
    order = list(range(row_bits))
    k = whole.shape[-1]
    sends = pick(whole, 1 - rbit[0], row_bits - 1).reshape(-1, k)
    keeps = pick(whole, rbit[0], row_bits - 1).reshape(-1, k)

    scaled = []
    for i in range(count):
        cols = basis[:, i * w : (i + 1) * w]
        left = list(reversed(order[1:]))
        shape = (2,) * len(left) + (block, w)
        away = jnp.dot(sends, cols, preferred_element_type=F32).astype(BF16)
        mine = jnp.dot(keeps, cols, preferred_element_type=F32).reshape(shape)
        for b in order[1:]:
            total = mine + swap(away, "row", n_row, b - 1).reshape(mine.shape).astype(F32)
            axis = left.index(b)
            away, mine = pick(total, 1 - rbit[b], axis).astype(BF16), pick(total, rbit[b], axis)
            left.remove(b)
        total = mine + swap(away, "row", n_row, order[-1]).reshape(mine.shape).astype(F32)
        part, have = (total / eigen[:, i * w : (i + 1) * w]).astype(BF16), []
        for b in reversed(order):
            got = swap(part, "row", n_row, b)
            have = sorted(have + [b], reverse=True)
            part = in_order(part, got, rbit[b], have.index(b))
        scaled.append(part.reshape(n_row * block, w))

    out = None
    for i in range(count):
        cols = basis[:, i * w : (i + 1) * w]
        term = lax.dot_general(scaled[i], cols, ALONG, preferred_element_type=F32)
        out = term if out is None else out + term
    out = out.reshape((2,) * col_bits + (gradient.shape[0], -1))
    left = list(reversed(range(col_bits)))
    for b in range(col_bits):
        axis = left.index(b)
        away, mine = pick(out, 1 - cbit[b], axis).astype(BF16), pick(out, cbit[b], axis)
        out = mine + swap(away, "col", n_col, b).astype(F32)
        left.remove(b)
    return out.astype(BF16)


def copy_block(sources, which, at, rows, to, slot):
    at = pl.multiple_of(at * rows, rows)
    for d, source in enumerate(sources):

        @pl.when(which == d)
        def _():
            to[pl.ds(slot * rows, rows), :] = source[pl.ds(at, rows), :]


DEPTH = 4


def stream(steps, fetch, work):
    def prime(_=None):
        for i in range(min(DEPTH - 1, steps)):
            fetch(i, i).start()

    def loop():
        def step(i, carry):
            slot = lax.rem(i, DEPTH)
            fetch(i, slot).wait()

            @pl.when(i + DEPTH - 1 < steps)
            def _():
                fetch(i + DEPTH - 1, lax.rem(i + DEPTH - 1, DEPTH)).start()

            work(i, slot)
            return carry

        lax.fori_loop(0, steps, step, 0)

    return prime, loop


def rotate_body(bits, block, n, start, tile, idx, *refs):
    shards, (b, away, keep, rows, ring, sems) = refs[:n], refs[n:]
    slots = 1 << len(bits)
    half = slots // 2 * block

    def fetch(i, slot):
        at = pl.multiple_of(start + i * tile, LANES)
        return pltpu.make_async_copy(b.at[:, pl.ds(at, tile)], ring.at[slot], sems.at[slot])

    def work(i, slot):
        out = jnp.dot(rows[...], ring[slot], preferred_element_type=F32)
        at = pl.ds(pl.multiple_of(i * tile, LANES), tile)
        keep[:, at] = out[:half]
        away[:, at] = out[half:].astype(BF16)

    prime, loop = stream(keep.shape[1] // tile, fetch, work)
    prime()
    for slot in range(slots):
        p = {bit: slot >> (len(bits) - 1 - j) & 1 for j, bit in enumerate(bits)}
        which = idx[1] ^ p[1]
        if 2 in p:
            which = which + 2 * (idx[2] ^ p[2])
        copy_block(shards, which, idx[0] ^ p[0], block, rows, slot)
    loop()


VMEM = pl.BlockSpec(memory_space=pltpu.VMEM)


def kernel(body, outs, scratch, aliases, flops, moved, limit, idx, basis_at, *args):
    specs = [pl.BlockSpec(memory_space=pltpu.SMEM)] + [VMEM] * len(args)
    specs[1 + basis_at] = pl.BlockSpec(memory_space=pl.ANY)
    return pl.pallas_call(
        body,
        in_specs=specs,
        out_specs=[VMEM] * len(outs),
        out_shape=outs,
        scratch_shapes=scratch + [pltpu.SemaphoreType.DMA((DEPTH,))],
        input_output_aliases=aliases,
        compiler_params=pltpu.CompilerParams(vmem_limit_bytes=limit),
        cost_estimate=pl.CostEstimate(flops=flops, bytes_accessed=moved, transcendentals=0),
    )(idx, *args)


def rotate(idx, shards, basis, start, w, bits, block):
    k = shards[0].shape[1]
    tile = tile_of(w, 256)
    count = block << len(bits)
    return kernel(
        functools.partial(rotate_body, bits, block, len(shards), start, tile),
        [jax.ShapeDtypeStruct((count // 2, w), x) for x in (BF16, F32)],
        [pltpu.VMEM((count, k), BF16), pltpu.VMEM((DEPTH, k, tile), BF16)],
        {},
        2 * count * k * w,
        2 * k * w,
        26 << 20,
        idx,
        len(shards),
        *shards,
        basis,
    )


def back_body(bits, block, more, start, tile, idx, lo, hi, b, *refs):
    parts = 1 << len(bits) - 1
    before = refs[:parts]
    outs, (rows, ring, sems) = refs[-3 - parts : -3], refs[-3:]
    w = lo.shape[1]

    def fetch(i, slot):
        at = pl.ds(pl.multiple_of(i * tile, tile), tile)
        return pltpu.make_async_copy(b.at[at, pl.ds(start, w)], ring.at[slot], sems.at[slot])

    def work(i, slot):
        out = lax.dot_general(rows[...], ring[slot], ALONG, preferred_element_type=F32)
        at = pl.ds(pl.multiple_of(i * tile, LANES), tile)
        for n in range(parts):
            part = out[2 * n * block : 2 * (n + 1) * block]
            if more:
                part = part + before[n][:, at]
            outs[n][:, at] = part.astype(outs[n].dtype)

    prime, loop = stream(b.shape[0] // tile, fetch, work)
    prime()
    for slot in range(2 * parts):
        p = {bit: idx[bit] ^ (slot >> bit & 1) for bit in bits}
        at = p[bits[1]] if len(bits) == 2 else 2 * p[bits[1]] + p[bits[2]]
        copy_block((lo, hi), p[bits[0]], at, block, rows, slot)
    loop()


def back(idx, lo, hi, basis, start, w, bits, block, before, last):
    k = basis.shape[0]
    tile = tile_of(k, 512)
    parts = 1 << len(bits) - 1
    kinds = [BF16 if last and n % 2 else F32 for n in range(parts)]
    return kernel(
        functools.partial(back_body, bits, block, len(before) > 0, start, tile),
        [jax.ShapeDtypeStruct((2 * block, k), x) for x in kinds],
        [pltpu.VMEM((2 * lo.shape[0], w), BF16), pltpu.VMEM((DEPTH, tile, w), BF16)],
        {4 + n: n for n in range(len(before)) if kinds[n] == F32},
        4 * lo.shape[0] * k * w,
        2 * k * w,
        26 << 20,
        idx,
        2,
        lo,
        hi,
        basis,
        *before,
    )


def columns(body, idx, ins, outs):
    w = outs[0].shape[1]
    tile = tile_of(w, 1792)
    specs = [
        pl.BlockSpec((x.shape[0], tile), functools.partial(lambda f, i, idx: (0, i + f), start // tile))
        for x, start in ins
    ]
    moved = sum(x.shape[0] * w * x.dtype.itemsize for x, _ in ins)
    return pl.pallas_call(
        body,
        grid_spec=pltpu.PrefetchScalarGridSpec(
            num_scalar_prefetch=1,
            grid=(w // tile,),
            in_specs=specs,
            out_specs=[pl.BlockSpec((o.shape[0], tile), lambda i, idx: (0, i)) for o in outs],
        ),
        out_shape=outs,
        compiler_params=pltpu.CompilerParams(vmem_limit_bytes=24 << 20),
        cost_estimate=pl.CostEstimate(flops=moved, bytes_accessed=2 * moved, transcendentals=0),
    )(idx, *[x for x, _ in ins])


def sum_body(idx, keep, got, away):
    away[...] = (keep[...] + got[...].astype(F32)).astype(BF16)


def three(keep, a, b, rows):
    return keep[rows, :] + a[rows, :].astype(F32) + b[rows, :].astype(F32)


def halve_body(idx, keep, got, more, keep2, away2):
    half = keep2.shape[0]
    keep2[...] = three(keep, got, more, slice(0, half))
    away2[...] = three(keep, got, more, slice(half, 2 * half)).astype(BF16)


def merge_body(idx, own, own_y, own_e, far, far_y, far_e, keep, away):
    a = three(own, own_y, own_e, slice(None))
    b = three(far, far_y, far_e, slice(None))
    straight = idx[2] == 0
    keep[...] = jnp.where(straight, a, b)
    away[...] = jnp.where(straight, b, a).astype(BF16)


def scale_body(idx, keep, got, mine, other, out):
    block = mine.shape[0]
    low = idx[3] == 0
    total = keep[...] + got[...].astype(F32)
    first = jnp.where(low, mine[...], other[...])
    second = jnp.where(low, other[...], mine[...])
    out[:block, :] = (total[:block] / first).astype(BF16)
    out[block:, :] = (total[block:] / second).astype(BF16)


def inner(idx, a, b):
    return jnp.where(idx[4] == 1, a[...], b[...])


def join_body(idx, near, away, near_out, away_out, out):
    half = near.shape[0]
    out[:half, :] = inner(idx, near, near_out)
    out[half:, :] = inner(idx, away, away_out)


def part_body(idx, near, away, near_out, away_out, own, far):
    a, b = inner(idx, near, near_out), inner(idx, away, away_out)
    straight = idx[2] == 0
    own[...] = jnp.where(straight, a, b)
    far[...] = jnp.where(straight, b, a)


def add_body(idx, keep, got, out):
    out[...] = (keep[...] + got[...].astype(F32)).astype(BF16)


def last_body(idx, keep, got, far, out):
    out[...] = (keep[...] + got[...].astype(F32) + far[...].astype(F32)).astype(BF16)


def paired(n_row, n_col, chunks, gradient, basis, eigen):
    r, c = lax.axis_index("row"), lax.axis_index("col")
    bits = [r & 1, c & 1, ((r >> 2) ^ (c >> 1)) & 1, (r >> 1) & 1, ((r >> 2) ^ (r >> 1)) & 1]
    idx = jnp.stack(bits).astype(jnp.int32)
    block = eigen.shape[0]
    starts, at = [], 0
    for part, _, _ in chunks:
        starts.append(at)
        at += eigen.shape[1] * part // PARTS
    widths = [b - a for a, b in zip(starts, starts[1:] + [at])]
    s = jax.ShapeDtypeStruct
    mid = [d for d in range(n_row) if (d >> 2 ^ d >> 1) & 1]
    inwards = [(d ^ 2, d) for d in mid]
    outwards = [(d, d ^ 2) for d in mid]
    across = [(d, d ^ 6) for d in mid]

    def send(x, pairs):
        return lax.ppermute(x, "row", pairs)

    def row(x):
        return swap(x, "row", n_row, 0)

    def col(x, bit):
        return swap(x, "col", n_col, bit)

    def cols(body, ins, outs):
        ins = [x if isinstance(x, tuple) else (x, 0) for x in ins]
        outs = [s((rows, ins[0][0].shape[1]), kind) for rows, kind in outs]
        out = columns(body, idx, ins, outs)
        return out if len(outs) > 1 else out[0]

    far_half = col(gradient, 1)
    shards = {"own": (gradient, col(gradient, 0)), "far": (far_half, col(far_half, 0))}
    other = send(eigen, inwards)

    def rotated(held, i, order):
        away, keep = rotate(idx, held, basis, starts[i], widths[i], order, block)
        got = row(away)
        total = cols(sum_body, [keep, got], [(keep.shape[0], BF16)])
        return [keep, got, send(total, inwards)]

    held = {}
    halves = [(2 * block, F32), (2 * block, BF16)]
    for i, (_, cut, _) in enumerate(chunks):
        if cut:
            part = rotated(shards["own"], i, (0, 1))
            part += rotated(shards["far"], i, (0, 1))
            keep, away = cols(merge_body, part, halves)
        else:
            part = rotated(shards["own"] + shards["far"], i, (0, 2, 1))
            keep, away = cols(halve_body, part, halves)
        got = send(away, across)
        held[i] = cols(scale_body, [keep, got, (eigen, starts[i]), (other, starts[i])], halves[1:])

    done = ()
    for i, (_, _, cut) in enumerate(chunks):
        near = held[i]
        away = send(near, across)
        near_out = send(near, outwards)
        parts = [near, away, near_out, send(away, outwards)]
        last = i == len(chunks) - 1
        if not cut:
            lo = cols(join_body, parts, [(4 * block, BF16)])
            hi = row(lo)
            done = back(idx, lo, hi, basis, starts[i], widths[i], (0, 2, 1), block, done, last)
            continue
        own, far = cols(part_body, parts, [(2 * block, BF16)] * 2)
        parts = []
        for lo, before in ((own, done[:2]), (far, done[2:])):
            hi = row(lo)
            parts += back(idx, lo, hi, basis, starts[i], widths[i], (0, 1), block, before, last)
        done = tuple(parts)

    def final(body, ins):
        outs = [s(gradient.shape, BF16)]
        return columns(body, idx, [(x, 0) for x in ins], outs)[0]

    far = final(add_body, [done[2], col(done[3], 0)])
    far = col(far, 1)
    return final(last_body, [done[0], col(done[1], 0), far])


CHUNKS = (
    (1, True, False),
    (1, True, False),
    (1, False, True),
    (1, False, True),
)
PARTS = sum(part for part, _, _ in CHUNKS)


def solution(mesh):
    n_row, n_col = mesh.shape["row"], mesh.shape["col"]
    fits = n_row == 2 * n_col and n_col.bit_length() == 3

    def per_device(gradient, basis, eigen):
        if fits:
            return paired(n_row, n_col, CHUNKS, gradient, basis, eigen)
        return general(n_row, n_col, gradient, basis, eigen)

    return jax.shard_map(
        per_device,
        mesh=mesh,
        in_specs=(P("col", "row"), P("row", "col"), P("row", "col")),
        out_specs=P("col", "row"),
        check_vma=False,
    )
```
